32 devices in a mesh: seq: 8 (over z, x), tp: 4 (over y, core).
Axes of the slice: x: 2, y: 2, z: 4, core: 2. Of those that a mesh axis runs over, the one named last changes fastest.
Arguments:
- tokens: bfloat16 [2048, 1536], P('seq'), may hold values from -6 to 6
- norm1_gain: bfloat16 [1536], replicated, may hold values from 0.25 to 1.75
- w_query: bfloat16 [1536, 1536], P('tp'), may hold values from -0.15625 to 0.15625
- key_weight: bfloat16 [512, 1536], P('tp'), may hold values from -0.4375 to 0.4375
- value_weight: bfloat16 [512, 1536], P('tp'), may hold values from -0.15625 to 0.15625
- rotated_key_cache: bfloat16 [4, 8, 524288], P(None, 'tp', 'seq'), may hold values from -60 to 60
- stored_value_cache: bfloat16 [4, 8, 524288], P(None, 'tp', 'seq'), may hold values from -6 to 6
- cache_len: int32 [4], replicated, may hold values from 1 to 8192, 16384 in all
- w_out: bfloat16 [1536, 1536], P('tp'), may hold values from -0.15625 to 0.15625
- norm2_gain: bfloat16 [1536], replicated, may hold values from 0.25 to 1.75
- w_router: bfloat16 [1536, 40], replicated, may hold values from -0.0546875 to 0.0546875
- expert_ids: int32 [2048, 8], P('seq'), may hold values from 0 to 39, all different within a row
- w_gate_up: bfloat16 [40, 2, 1536, 512], P('tp', None, 'seq'), may hold values from -0.15625 to 0.15625
- w_down: bfloat16 [40, 512, 1536], P('tp', 'seq'), may hold values from -0.5 to 0.5
Outputs:
- attn_out: bfloat16 [2048, 1536], P('seq')
- expert_out: bfloat16 [2048, 1536], P('seq')
The draws below stay inside these ranges and needn't reach their ends.
Inputs may be any that keep to these rules, and one draw needn't show every extreme that they name: `cache_len`: request lengths of 1 to 8192; one request fills all 8192 positions. `expert_ids`: each row names 8 different experts; every expert is named.
All inputs are finite; a program needn't handle non-finite values.
Results may differ from the reference program's by a relative error of at most 0.03.
Values may be sent and summed in bfloat16 or wider, within the bound.
A program may use at most 192 MiB of HBM per device.

```python
import math
import jax
import jax.numpy as jnp
import numpy as np
from jax import lax

MODEL_WIDTH = 1536
QUERY_HEADS = 24
KEY_VALUE_HEADS = 8
HEAD_SIZE = 64
EXPERTS = 40
FFE = 512
TOPK = 8
FRESH_TOKENS = 512
CACHE_LENGTH = 8192
REQUEST_COUNT = 4
TOKENS = 2048


def draw_rotated_key_cache(key, part):
    array_shape = (REQUEST_COUNT, KEY_VALUE_HEADS, CACHE_LENGTH, HEAD_SIZE)
    base_values = jnp.clip(3.0 * jax.random.normal(key, array_shape, jnp.float32), -18.0, 18.0)
    magnitude = jax.random.uniform(jax.random.fold_in(key, 31), (REQUEST_COUNT, KEY_VALUE_HEADS, 1, HEAD_SIZE), jnp.float32, 45.0, 57.0)
    signs = jnp.where(jax.random.bernoulli(jax.random.fold_in(key, 37), 0.5, (REQUEST_COUNT, KEY_VALUE_HEADS, 1, HEAD_SIZE)), 1.0, -1.0)
    loud_key = magnitude * signs
    spot = jax.random.randint(jax.random.fold_in(key, 41), (REQUEST_COUNT, 1, 1, 1), 2, CACHE_LENGTH - 1)
    where_pos = jnp.arange(CACHE_LENGTH, dtype=jnp.int32)[None, None, :, None]
    first_loud = (where_pos == 0) | (where_pos == spot)
    second_loud = (where_pos == 1) | (where_pos == spot + 1)
    factor = jnp.where(first_loud, 1.0, jnp.where(second_loud, 1.02, 0.0))
    mixed = jnp.where(factor > 0.0, loud_key * factor, base_values)
    return mixed.reshape(REQUEST_COUNT, KEY_VALUE_HEADS, CACHE_LENGTH * HEAD_SIZE).astype(jnp.bfloat16)


def block_scale(rng, dims, split, least, high):
    def one(axis_at, parts):
        heights = jax.random.uniform(jax.random.fold_in(jax.random.fold_in(rng, 6), axis_at), (parts,), jnp.float32, least / len(split), high / len(split))
        return jnp.repeat(jnp.exp(heights), dims[axis_at] // parts).reshape((-1,) + (1,) * (len(dims) - axis_at - 1))

    factor_of = one(*split[0])
    for cut in split[1:]:
        factor_of = factor_of * one(*cut)
    return factor_of


def different_ones(stream_key, rows, count, top, lift):
    sequence = jax.random.permutation(jax.random.fold_in(stream_key, 1), count)
    boost = sequence
    for power in range(3):
        boost = boost * boost // count
    boost = boost * lift // count
    chance = jax.random.randint(jax.random.fold_in(stream_key, 2), (rows, count), 0, 4096) + boost
    sure = jax.random.permutation(jax.random.fold_in(stream_key, 3), rows)[jnp.arange(count) % rows]
    chance = jnp.where(jnp.arange(rows)[:, None] == sure[None, :], 1 << 14, chance)
    merit = chance * count + jnp.arange(count)
    return lax.top_k(merit.astype(jnp.int32), top)[1].astype(jnp.int32)


def split_up(amount, total, most, slope):
    loads = [(1 << 20) // math.isqrt(standing ** slope) + 1 for standing in range(2, amount + 1)]
    rest, counts = total - most - (amount - 1), [1] * (amount - 1)
    while rest > 0:
        movable = [i for i in range(amount - 1) if counts[i] < most]
        pool, budget = sum([loads[i] for i in movable]), rest
        for i in movable:
            more = min(most - counts[i], max(1, budget * loads[i] // pool), rest)
            counts[i] = counts[i] + more
            rest = rest - more
    return np.array([most] + counts)


def uneven_parts(stream_key, count, total, bound, skew):
    if count == 2:
        one = jax.random.randint(stream_key, (), max(1, total - bound), min(bound, total - 1) + 1)
        return jnp.stack([one, total - one])
    sizes = jnp.asarray(split_up(count, total, bound, skew), jnp.int32)
    twos = (count - 1) // 2
    source_of, taker = sizes[1:1 + 2 * twos:2], sizes[2:2 + 2 * twos:2]
    slack = jnp.minimum(source_of - 1, bound - taker)
    passed = jax.random.randint(jax.random.fold_in(stream_key, 1), (twos,), 0, 1 << 20) % (slack + 1)
    sizes = sizes.at[1:1 + 2 * twos:2].set(source_of - passed).at[2:2 + 2 * twos:2].set(taker + passed)
    return sizes[jax.random.permutation(jax.random.fold_in(stream_key, 2), count)]


def gaussian(key, dims, deviation, limit, shards=(), kind=jnp.bfloat16):
    values = deviation * jax.random.normal(key, dims, jnp.float32)
    if shards:
        values = values * block_scale(key, dims, shards, -0.22, 0.18)
    return jnp.clip(values, -limit, limit).astype(kind)


def setup_inputs(seed: int = 0) -> dict:
    splits = jax.random.split(jax.random.key(seed), 15)
    tokens = gaussian(splits[0], (TOKENS, MODEL_WIDTH), 1.0, 6.0, ((0, 8),))
    norm1_gain = jnp.clip(1.0 + 0.15 * jax.random.normal(splits[1], (MODEL_WIDTH,), jnp.float32), 0.25, 1.75).astype(jnp.bfloat16)
    w_query = gaussian(splits[2], (QUERY_HEADS * HEAD_SIZE, MODEL_WIDTH), MODEL_WIDTH ** -0.5, 0.15625, ((0, 4),))
    key_weight = gaussian(splits[3], (KEY_VALUE_HEADS * HEAD_SIZE, MODEL_WIDTH), (MODEL_WIDTH // 9) ** -0.5, 0.4375, ((0, 4),))
    value_weight = gaussian(splits[4], (KEY_VALUE_HEADS * HEAD_SIZE, MODEL_WIDTH), MODEL_WIDTH ** -0.5, 0.15625, ((0, 4),))
    rotated_key_cache = draw_rotated_key_cache(jax.random.fold_in(splits[14], 71), 0)
    stored_value_cache = gaussian(splits[6], (REQUEST_COUNT, KEY_VALUE_HEADS, CACHE_LENGTH * HEAD_SIZE), 1.0, 6.0, ((1, 4), (2, 8)))
    cache_len = uneven_parts(splits[7], REQUEST_COUNT, REQUEST_COUNT * CACHE_LENGTH // 2, CACHE_LENGTH, 2).astype(jnp.int32)
    w_out = gaussian(splits[8], (QUERY_HEADS * HEAD_SIZE, MODEL_WIDTH), (QUERY_HEADS * HEAD_SIZE) ** -0.5, 0.15625, ((0, 4),))
    norm2_gain = jnp.clip(1.0 + 0.15 * jax.random.normal(splits[9], (MODEL_WIDTH,), jnp.float32), 0.25, 1.75).astype(jnp.bfloat16)
    w_router = gaussian(splits[10], (MODEL_WIDTH, EXPERTS), (MODEL_WIDTH * 8) ** -0.5, 0.0546875)
    expert_ids = different_ones(splits[11], TOKENS, EXPERTS, TOPK, 3276)
    w_gate_up = gaussian(splits[12], (EXPERTS, 2, MODEL_WIDTH, FFE), MODEL_WIDTH ** -0.5, 0.15625, ((0, 4), (2, 8)))
    w_down = gaussian(splits[13], (EXPERTS, FFE, MODEL_WIDTH), (FFE // 4) ** -0.5, 0.5, ((0, 4), (1, 8)))
    return {"tokens": tokens, "norm1_gain": norm1_gain, "w_query": w_query, "key_weight": key_weight, "value_weight": value_weight, "rotated_key_cache": rotated_key_cache, "stored_value_cache": stored_value_cache, "cache_len": cache_len, "w_out": w_out, "norm2_gain": norm2_gain, "w_router": w_router, "expert_ids": expert_ids, "w_gate_up": w_gate_up, "w_down": w_down}


EPS = 1e-05
THETA = 10000.0

def rms_norm(values, gain):
    mean_square = lax.optimization_barrier(jnp.mean(values * values, axis=-1, keepdims=True))
    return values * lax.rsqrt(mean_square + EPS) * gain.astype(values.dtype)

def apply_rotary(values, positions):
    half_dim = values.shape[-1] // 2
    exponent = jnp.arange(half_dim, dtype=jnp.float32) * (2.0 / values.shape[-1])
    freqs = THETA ** (-exponent)
    angles = positions[:, None] * freqs[None, :]
    cosine = jnp.cos(angles)[:, None, :]
    sine = jnp.sin(angles)[:, None, :]
    first = values[..., :half_dim]
    second = values[..., half_dim:]
    return jnp.concatenate([first * cosine - second * sine, second * cosine + first * sine], axis=-1)

def apply_projection(normalized_input, weight):
    return jnp.einsum('td,fd->tf', normalized_input, weight, preferred_element_type=jnp.float32)

def reference(tokens, norm1_gain, w_query, key_weight, value_weight, rotated_key_cache, stored_value_cache, cache_len, w_out, norm2_gain, w_router, expert_ids, w_gate_up, w_down):
    token_count = tokens.shape[0]
    query_group = QUERY_HEADS // KEY_VALUE_HEADS
    scale = HEAD_SIZE ** (-0.5)
    inputs = tokens.astype(jnp.float32)
    normalized_input = rms_norm(inputs, norm1_gain).astype(jnp.bfloat16)
    row_ids = jnp.arange(token_count, dtype=jnp.int32)
    owners = row_ids // FRESH_TOKENS
    positions = (cache_len[owners] + row_ids % FRESH_TOKENS).astype(jnp.int32)
    angle_position = positions.astype(jnp.float32)
    query_vector = apply_rotary(apply_projection(normalized_input, w_query).reshape(token_count, QUERY_HEADS, HEAD_SIZE), angle_position).astype(jnp.bfloat16)
    fresh_key = apply_rotary(apply_projection(normalized_input, key_weight).reshape(token_count, KEY_VALUE_HEADS, HEAD_SIZE), angle_position).astype(jnp.bfloat16)
    fresh_value = apply_projection(normalized_input, value_weight).astype(jnp.bfloat16).reshape(token_count, KEY_VALUE_HEADS, HEAD_SIZE)
    cache_pos = jnp.arange(CACHE_LENGTH, dtype=jnp.int32)

    def one_request(request_index):
        length = lax.dynamic_index_in_dim(cache_len, request_index, 0, keepdims=False)
        start_position = (request_index * FRESH_TOKENS).astype(jnp.int32)
        query_rows = lax.dynamic_slice_in_dim(query_vector, start_position, FRESH_TOKENS, 0).reshape(FRESH_TOKENS, KEY_VALUE_HEADS, query_group, HEAD_SIZE).astype(jnp.float32)
        query_pos = length + jnp.arange(FRESH_TOKENS, dtype=jnp.int32)
        prior_keys = jnp.transpose(lax.dynamic_index_in_dim(rotated_key_cache, request_index, 0, keepdims=False).reshape(KEY_VALUE_HEADS, CACHE_LENGTH, HEAD_SIZE), (1, 0, 2))
        prior_values = jnp.transpose(lax.dynamic_index_in_dim(stored_value_cache, request_index, 0, keepdims=False).reshape(KEY_VALUE_HEADS, CACHE_LENGTH, HEAD_SIZE), (1, 0, 2))
        keys = jnp.concatenate([prior_keys, lax.dynamic_slice_in_dim(fresh_key, start_position, FRESH_TOKENS, 0)], axis=0).astype(jnp.float32)
        values = jnp.concatenate([prior_values, lax.dynamic_slice_in_dim(fresh_value, start_position, FRESH_TOKENS, 0)], axis=0).astype(jnp.float32)
        key_pos = jnp.concatenate([cache_pos, query_pos])
        usable = jnp.concatenate([cache_pos < length, jnp.ones((FRESH_TOKENS,), dtype=bool)])
        allowed = usable[None, :] & (key_pos[None, :] <= query_pos[:, None])

        def single_head(head):
            head_q = lax.dynamic_index_in_dim(query_rows, head, 1, keepdims=False)
            head_k = lax.dynamic_index_in_dim(keys, head, 1, keepdims=False)
            head_v = lax.dynamic_index_in_dim(values, head, 1, keepdims=False)
            scores = jnp.einsum('ngd,kd->gnk', head_q, head_k) * scale
            scores = jnp.where(allowed[None], scores, -jnp.inf)
            peak = lax.optimization_barrier(jnp.max(scores, axis=-1, keepdims=True))
            weights = jnp.where(allowed[None], jnp.exp(scores - peak), 0.0)
            total = lax.optimization_barrier(jnp.sum(weights, axis=-1))
            mixed = jnp.einsum('gnk,kd->ngd', weights.astype(jnp.bfloat16).astype(jnp.float32), head_v)
            return mixed / jnp.transpose(total, (1, 0))[:, :, None]
        head_list = lax.map(single_head, jnp.arange(KEY_VALUE_HEADS, dtype=jnp.int32))
        return jnp.transpose(head_list, (1, 0, 2, 3)).reshape(FRESH_TOKENS, QUERY_HEADS * HEAD_SIZE).astype(jnp.bfloat16)
    attention = lax.map(one_request, jnp.arange(REQUEST_COUNT, dtype=jnp.int32)).reshape(token_count, QUERY_HEADS * HEAD_SIZE)
    attn = jnp.dot(attention, w_out, preferred_element_type=jnp.float32)
    attn_out = attn.astype(jnp.bfloat16)
    normed2 = rms_norm(inputs + attn, norm2_gain).astype(jnp.bfloat16)
    logits = jnp.dot(normed2, w_router, preferred_element_type=jnp.float32)
    chosen = jnp.take_along_axis(logits, expert_ids, axis=1)
    gates = jax.nn.softmax(chosen, axis=-1)
    picked = expert_ids[:, :, None] == jnp.arange(EXPERTS, dtype=jnp.int32)[None, None, :]
    share = lax.optimization_barrier(jnp.sum(jnp.where(picked, gates[:, :, None], 0.0), axis=1))

    def one_expert(running, expert):
        both = lax.dynamic_index_in_dim(w_gate_up, expert, 0, keepdims=False)
        gate = jnp.dot(normed2, both[0], preferred_element_type=jnp.float32)
        upward = jnp.dot(normed2, both[1], preferred_element_type=jnp.float32)
        column = lax.dynamic_index_in_dim(share, expert, 1, keepdims=True)
        hidden = (jax.nn.silu(gate) * upward * column).astype(jnp.bfloat16)
        down = lax.dynamic_index_in_dim(w_down, expert, 0, keepdims=False)
        return (running + jnp.dot(hidden, down, preferred_element_type=jnp.float32), None)
    moe, unused = lax.scan(one_expert, jnp.zeros((token_count, MODEL_WIDTH), jnp.float32), jnp.arange(EXPERTS, dtype=jnp.int32))
    return (attn_out, moe.astype(jnp.bfloat16))
```

```python
import jax
import jax.numpy as jnp
from jax import lax
from jax.experimental import pallas as pl
from jax.experimental.pallas import tpu as pltpu
from jax.sharding import PartitionSpec as P

HEAD_SIZE = 64
FRESH_TOKENS = 512


EPS = 1e-05
THETA = 10000.0
NEGATIVE = -1e30


def rms_norm(values, gain):
    mean_square = jnp.mean(values * values, axis=-1, keepdims=True)
    return values * lax.rsqrt(mean_square + EPS) * gain.astype(values.dtype)


def apply_rotary(values, positions):
    half_dim = values.shape[-1] // 2
    exponent = jnp.arange(half_dim, dtype=jnp.float32) * (2.0 / values.shape[-1])
    freqs = THETA ** (-exponent)
    angles = positions[:, None] * freqs[None, :]
    cosine = jnp.cos(angles)[:, None, :]
    sine = jnp.sin(angles)[:, None, :]
    first = values[..., :half_dim]
    second = values[..., half_dim:]
    return jnp.concatenate(
        [first * cosine - second * sine, second * cosine + first * sine], axis=-1
    )


def apply_projection(normalized_input, weight):
    return jnp.einsum("td,fd->tf", normalized_input, weight, preferred_element_type=jnp.float32)


def lookup(table, index):
    hits = index[:, None] == jnp.arange(table.shape[0], dtype=jnp.int32)[None, :]
    return jnp.sum(jnp.where(hits, table[None, :], 0), axis=1)


def attend_kernel(info, q_ref, k_ref, v_ref, fk_ref, fv_ref, out_ref, peak_ref, sum_ref, acc_ref):
    group, rows = out_ref.shape[1], out_ref.shape[2]
    pairs = k_ref.shape[2]
    columns = q_ref.shape[1]
    head = pl.program_id(0)
    dest = pl.program_id(1)
    me = info[0]
    per = FRESH_TOKENS // rows
    length = info[1 + dest // per]
    base = me * (2 * pairs)
    col = lax.broadcasted_iota(jnp.int32, (columns, 128), 0)
    lane = lax.broadcasted_iota(jnp.int32, (columns, 128), 1)
    out_lane = lax.broadcasted_iota(jnp.int32, (rows, 128), 1)
    has_cache = base < length
    has_fresh = (dest // per == me // per) & (dest >= me)
    nt = (((1,), (1,)), ((), ()))

    def pick(g, odd):
        start = (head * group + g) * HEAD_SIZE
        hit = (col == start + lane - odd * HEAD_SIZE) & (lane // HEAD_SIZE == odd)
        select = jnp.where(hit, HEAD_SIZE ** (-0.5), 0.0).astype(jnp.bfloat16)
        return jnp.dot(q_ref[...], select, preferred_element_type=jnp.float32).astype(jnp.bfloat16)

    @pl.when(jnp.logical_not(has_cache))
    def _():
        peak_ref[...] = jnp.full_like(peak_ref, NEGATIVE)
        sum_ref[...] = jnp.zeros_like(sum_ref)
        acc_ref[...] = jnp.zeros_like(acc_ref)

    @pl.when(has_cache)
    def _():
        keys = k_ref[0, 0]
        values = v_ref[0, 0]
        even_pos = base + 2 * lax.broadcasted_iota(jnp.int32, (1, pairs), 1)
        even_bias = jnp.where(even_pos < length, 0.0, NEGATIVE)
        odd_bias = jnp.where(even_pos + 1 < length, 0.0, NEGATIVE)
        for g in range(group):
            even = lax.dot_general(pick(g, 0), keys, nt, preferred_element_type=jnp.float32) + even_bias
            odd = lax.dot_general(pick(g, 1), keys, nt, preferred_element_type=jnp.float32) + odd_bias
            peak = jnp.max(jnp.maximum(even, odd), axis=1, keepdims=True)
            even = jnp.exp(even - peak)
            odd = jnp.exp(odd - peak)
            total = jnp.sum(even + odd, axis=1, keepdims=True)
            mix_even = jnp.dot(even.astype(jnp.bfloat16), values, preferred_element_type=jnp.float32)
            mix_odd = jnp.dot(odd.astype(jnp.bfloat16), values, preferred_element_type=jnp.float32)
            mixed = jnp.where(out_lane < HEAD_SIZE, mix_even, mix_odd)
            peak_ref[g] = jnp.broadcast_to(peak, (rows, 128))
            sum_ref[g] = jnp.broadcast_to(total, (rows, 128))
            acc_ref[g] = mixed

    @pl.when(has_fresh)
    def _():
        row_q = dest * rows + lax.broadcasted_iota(jnp.int32, (rows, rows), 0)
        row_k = me * rows + lax.broadcasted_iota(jnp.int32, (rows, rows), 1)
        bias = jnp.where(row_k <= row_q, 0.0, NEGATIVE)
        for g in range(group):
            score = lax.dot_general(pick(g, 0), fk_ref[0], nt, preferred_element_type=jnp.float32) + bias
            old = peak_ref[g][:, :1]
            peak = jnp.maximum(old, jnp.max(score, axis=1, keepdims=True))
            weight = jnp.exp(score - peak)
            factor = jnp.exp(old - peak)
            total = sum_ref[g][:, :1] * factor + jnp.sum(weight, axis=1, keepdims=True)
            mix = jnp.dot(weight.astype(jnp.bfloat16), fv_ref[0], preferred_element_type=jnp.float32)
            acc_ref[g] = acc_ref[g] * factor + mix
            peak_ref[g] = jnp.broadcast_to(peak, (rows, 128))
            sum_ref[g] = jnp.broadcast_to(total, (rows, 128))

    for g in range(group):
        acc = acc_ref[g]
        acc = acc + pltpu.roll(acc, HEAD_SIZE, 1)
        total = sum_ref[g]
        some = total > 0.0
        safe = jnp.where(some, total, 1.0)
        level = jnp.where(some, peak_ref[g] + jnp.log(safe), NEGATIVE)
        high = level.astype(jnp.bfloat16).astype(jnp.float32)
        middle = (level - high).astype(jnp.bfloat16).astype(jnp.float32)
        low = level - high - middle
        tail = jnp.where(out_lane == HEAD_SIZE, high, jnp.where(out_lane == HEAD_SIZE + 1, middle, low))
        out_ref[0, g] = jnp.where(out_lane < HEAD_SIZE, acc / safe, tail).astype(out_ref.dtype)


def attend(info, query, keys, values, fresh_key, fresh_value, rows, local_q):
    local_kv, pairs = keys.shape[1], keys.shape[2]
    group = local_q // local_kv
    per = FRESH_TOKENS // rows
    dests = query.shape[0] // rows
    cache_spec = pl.BlockSpec((1, 1, pairs, 128), lambda j, d, info: (d // per, j, 0, 0))
    fresh_spec = pl.BlockSpec((1, rows, 128), lambda j, d, info: (j, 0, 0))
    return pl.pallas_call(
        attend_kernel,
        grid_spec=pltpu.PrefetchScalarGridSpec(
            num_scalar_prefetch=1,
            grid=(local_kv, dests),
            in_specs=[
                pl.BlockSpec((rows, local_q * HEAD_SIZE), lambda j, d, info: (d, 0)),
                cache_spec,
                cache_spec,
                fresh_spec,
                fresh_spec,
            ],
            out_specs=pl.BlockSpec((1, group, rows, 128), lambda j, d, info: (d, j, 0, 0)),
            scratch_shapes=[pltpu.VMEM((group, rows, 128), jnp.float32)] * 3,
        ),
        out_shape=jax.ShapeDtypeStruct((dests, local_q, rows, 128), jnp.bfloat16),
        compiler_params=pltpu.CompilerParams(vmem_limit_bytes=40 * 1024 * 1024),
        cost_estimate=pl.CostEstimate(
            flops=8 * query.size * pairs * 2, bytes_accessed=16 << 20, transcendentals=query.size * pairs // 32
        ),
    )(info, query, keys, values, fresh_key, fresh_value)


def per_device(
    tokens,
    norm1_gain,
    w_query,
    key_weight,
    value_weight,
    rotated_key_cache,
    stored_value_cache,
    cache_len,
    w_out,
    norm2_gain,
    w_router,
    expert_ids,
    w_gate_up,
    w_down,
):
    tok_rows, width = tokens.shape
    seq_pos = lax.axis_index("seq")
    tp_pos = lax.axis_index("tp")
    local_q = w_query.shape[0] // HEAD_SIZE
    local_kv = key_weight.shape[0] // HEAD_SIZE
    requests = rotated_key_cache.shape[0]
    span = rotated_key_cache.shape[2] // HEAD_SIZE
    inputs = tokens.astype(jnp.float32)
    devices = lax.axis_size("seq")
    local_experts, _, own_width, hidden_size = w_gate_up.shape
    own_hidden = hidden_size // devices
    own_gate_up = jnp.transpose(
        w_gate_up.reshape(local_experts, 2, own_width, devices, own_hidden), (3, 2, 1, 0, 4)
    ).reshape(width, 2 * local_experts * own_hidden)
    own_gate_up = lax.all_to_all(own_gate_up, "seq", 0, 0, tiled=True)
    normalized_input = rms_norm(inputs, norm1_gain).astype(jnp.bfloat16)
    row_ids = seq_pos * tok_rows + jnp.arange(tok_rows, dtype=jnp.int32)
    owners = row_ids // FRESH_TOKENS
    positions = lookup(cache_len, owners) + row_ids % FRESH_TOKENS
    angle_position = positions.astype(jnp.float32)
    query_vector = apply_rotary(
        apply_projection(normalized_input, w_query).reshape(tok_rows, local_q, HEAD_SIZE),
        angle_position,
    ).astype(jnp.bfloat16)
    fresh_key = apply_rotary(
        apply_projection(normalized_input, key_weight).reshape(tok_rows, local_kv, HEAD_SIZE),
        angle_position,
    ).astype(jnp.bfloat16)
    fresh_value = (
        apply_projection(normalized_input, value_weight)
        .astype(jnp.bfloat16)
        .reshape(tok_rows, local_kv, HEAD_SIZE)
    )
    all_query = lax.all_gather(
        query_vector.reshape(tok_rows, local_q * HEAD_SIZE), "seq", axis=0, tiled=True
    )
    paired = (requests, local_kv, span // 2, 2 * HEAD_SIZE)
    pad = ((0, 0), (0, 0), (0, HEAD_SIZE))
    parts = attend(
        jnp.concatenate([seq_pos[None].astype(jnp.int32), cache_len]),
        all_query,
        rotated_key_cache.reshape(paired),
        stored_value_cache.reshape(paired),
        jnp.pad(jnp.transpose(fresh_key, (1, 0, 2)), pad),
        jnp.pad(jnp.transpose(fresh_value, (1, 0, 2)), pad),
        tok_rows,
        local_q,
    )
    parts = lax.all_to_all(parts, "seq", 0, 0, tiled=True).astype(jnp.float32)
    level = jnp.sum(parts[..., HEAD_SIZE : HEAD_SIZE + 3], axis=-1, keepdims=True)
    factor = jnp.exp(level - jnp.max(level, axis=0, keepdims=True))
    heads_out = jnp.sum(parts[..., :HEAD_SIZE] * factor, axis=0) / jnp.sum(factor, axis=0)
    attn_part = jnp.einsum(
        "htd,hdf->tf",
        heads_out.astype(jnp.bfloat16),
        w_out.reshape(local_q, HEAD_SIZE, width),
        preferred_element_type=jnp.float32,
    )
    attn = lax.psum(attn_part.astype(jnp.bfloat16), "tp").astype(jnp.float32)
    attn_out = attn.astype(jnp.bfloat16)
    normed2 = rms_norm(inputs + attn, norm2_gain).astype(jnp.bfloat16)
    logits = jnp.dot(normed2, w_router, preferred_element_type=jnp.float32)
    experts_all = w_router.shape[1]
    picked_all = expert_ids[:, :, None] == jnp.arange(experts_all, dtype=jnp.int32)[None, None, :]
    chosen = jnp.sum(jnp.where(picked_all, logits[:, None, :], 0.0), axis=-1)
    gates = jax.nn.softmax(chosen, axis=-1)
    local_ids = tp_pos * local_experts + jnp.arange(local_experts, dtype=jnp.int32)
    picked = expert_ids[:, :, None] == local_ids[None, None, :]
    share = jnp.sum(jnp.where(picked, gates[:, :, None], 0.0), axis=1)
    share_high = lax.reduce_precision(share, 8, 7)
    packed = jnp.concatenate(
        [
            normed2,
            share_high.astype(jnp.bfloat16),
            (share - share_high).astype(jnp.bfloat16),
            jnp.zeros((tok_rows, 128 - 2 * local_experts), jnp.bfloat16),
        ],
        axis=1,
    )
    packed = lax.all_gather(packed, "seq", axis=0, tiled=True)
    units = local_experts * own_hidden
    unit_expert = jnp.arange(units, dtype=jnp.int32) // own_hidden
    lanes = jnp.arange(128, dtype=jnp.int32)
    spread = (lanes[:, None] % local_experts == unit_expert[None, :]) & (lanes[:, None] < 2 * local_experts)
    share_all = jnp.dot(packed[:, width:], spread.astype(jnp.bfloat16), preferred_element_type=jnp.float32)
    both = jnp.dot(packed[:, :width], own_gate_up, preferred_element_type=jnp.float32)
    hidden = (jax.nn.silu(both[:, :units]) * both[:, units:] * share_all).astype(jnp.bfloat16)
    moe_part = jnp.dot(hidden, w_down.reshape(units, width), preferred_element_type=jnp.float32)
    moe_part = lax.psum_scatter(moe_part.astype(jnp.bfloat16), "seq", scatter_dimension=0, tiled=True)
    expert_out = lax.psum(moe_part, "tp")
    return (attn_out, expert_out)


def solution(mesh):
    return jax.shard_map(
        per_device,
        mesh=mesh,
        in_specs=(
            P("seq", None),
            P(),
            P("tp", None),
            P("tp", None),
            P("tp", None),
            P(None, "tp", "seq"),
            P(None, "tp", "seq"),
            P(),
            P("tp", None),
            P(),
            P(),
            P("seq", None),
            P("tp", None, "seq", None),
            P("tp", "seq", None),
        ),
        out_specs=(P("seq", None), P("seq", None)),
        check_vma=False,
    )
```

```python
import functools

import jax
import jax.numpy as jnp
from jax import lax
from jax.experimental import pallas as pl
from jax.experimental.pallas import tpu as pltpu
from jax.sharding import PartitionSpec as P

HEAD_SIZE = 64
FRESH_TOKENS = 512


EPS = 1e-05
THETA = 10000.0
NEGATIVE = -1e30


def rms_norm(values, gain):
    mean_square = jnp.mean(values * values, axis=-1, keepdims=True)
    return values * lax.rsqrt(mean_square + EPS) * gain.astype(values.dtype)


def apply_rotary(values, positions):
    half_dim = values.shape[-1] // 2
    exponent = jnp.arange(half_dim, dtype=jnp.float32) * (2.0 / values.shape[-1])
    freqs = THETA ** (-exponent)
    angles = positions[:, None] * freqs[None, :]
    cosine = jnp.cos(angles)[:, None, :]
    sine = jnp.sin(angles)[:, None, :]
    first = values[..., :half_dim]
    second = values[..., half_dim:]
    return jnp.concatenate(
        [first * cosine - second * sine, second * cosine + first * sine], axis=-1
    )


def apply_projection(normalized_input, weight):
    return jnp.einsum("td,fd->tf", normalized_input, weight, preferred_element_type=jnp.float32)


def lookup(table, index):
    hits = index[:, None] == jnp.arange(table.shape[0], dtype=jnp.int32)[None, :]
    return jnp.sum(jnp.where(hits, table[None, :], 0), axis=1)


def attend_kernel(group, info, q_ref, k_ref, v_ref, fk_ref, fv_ref, out_ref, peak_ref, sum_ref, acc_ref):
    heads, rows = acc_ref.shape[0], acc_ref.shape[1]
    pairs = k_ref.shape[2]
    columns = q_ref.shape[1]
    dest = pl.program_id(0)
    me = info[0]
    per = FRESH_TOKENS // rows
    length = info[1 + dest // per]
    base = me * (2 * pairs)
    col = lax.broadcasted_iota(jnp.int32, (columns, 128), 0)
    lane = lax.broadcasted_iota(jnp.int32, (columns, 128), 1)
    out_lane = lax.broadcasted_iota(jnp.int32, (rows, 128), 1)
    has_cache = base < length
    has_fresh = (dest // per == me // per) & (dest >= me)
    nt = (((1,), (1,)), ((), ()))

    def pick(g, odd):
        hit = (col == g * HEAD_SIZE + lane - odd * HEAD_SIZE) & (lane // HEAD_SIZE == odd)
        select = jnp.where(hit, HEAD_SIZE ** (-0.5), 0.0).astype(jnp.bfloat16)
        return jnp.dot(q_ref[...], select, preferred_element_type=jnp.float32).astype(jnp.bfloat16)

    @pl.when(jnp.logical_not(has_cache))
    def _():
        peak_ref[...] = jnp.full_like(peak_ref, NEGATIVE)
        sum_ref[...] = jnp.zeros_like(sum_ref)
        acc_ref[...] = jnp.zeros_like(acc_ref)

    @pl.when(has_cache)
    def _():
        even_pos = base + 2 * lax.broadcasted_iota(jnp.int32, (1, pairs), 1)
        even_bias = jnp.where(even_pos < length, 0.0, NEGATIVE)
        odd_bias = jnp.where(even_pos + 1 < length, 0.0, NEGATIVE)
        @pl.loop(0, heads // group)
        def _(j):
            for i in range(group):
                g = j * group + i
                keys = k_ref[0, j]
                values = v_ref[0, j]
                even = lax.dot_general(pick(g, 0), keys, nt, preferred_element_type=jnp.float32) + even_bias
                odd = lax.dot_general(pick(g, 1), keys, nt, preferred_element_type=jnp.float32) + odd_bias
                peak = jnp.max(jnp.maximum(even, odd), axis=1, keepdims=True)
                even = jnp.exp(even - peak)
                odd = jnp.exp(odd - peak)
                total = jnp.sum(even + odd, axis=1, keepdims=True)
                mix_even = jnp.dot(even.astype(jnp.bfloat16), values, preferred_element_type=jnp.float32)
                mix_odd = jnp.dot(odd.astype(jnp.bfloat16), values, preferred_element_type=jnp.float32)
                mixed = jnp.where(out_lane < HEAD_SIZE, mix_even, mix_odd)
                peak_ref[g] = jnp.broadcast_to(peak, (rows, 128))
                sum_ref[g] = jnp.broadcast_to(total, (rows, 128))
                acc_ref[g] = mixed

    @pl.when(has_fresh)
    def _():
        row_q = dest * rows + lax.broadcasted_iota(jnp.int32, (rows, rows), 0)
        row_k = me * rows + lax.broadcasted_iota(jnp.int32, (rows, rows), 1)
        bias = jnp.where(row_k <= row_q, 0.0, NEGATIVE)
        @pl.loop(0, heads // group)
        def _(j):
            for i in range(group):
                g = j * group + i
                score = lax.dot_general(pick(g, 0), fk_ref[j], nt, preferred_element_type=jnp.float32) + bias
                old = peak_ref[g][:, :1]
                peak = jnp.maximum(old, jnp.max(score, axis=1, keepdims=True))
                weight = jnp.exp(score - peak)
                factor = jnp.exp(old - peak)
                total = sum_ref[g][:, :1] * factor + jnp.sum(weight, axis=1, keepdims=True)
                mix = jnp.dot(weight.astype(jnp.bfloat16), fv_ref[j], preferred_element_type=jnp.float32)
                acc_ref[g] = acc_ref[g] * factor + mix
                peak_ref[g] = jnp.broadcast_to(peak, (rows, 128))
                sum_ref[g] = jnp.broadcast_to(total, (rows, 128))

    tail = jnp.zeros((rows, 128), jnp.float32)
    left = None
    for g in range(heads):
        acc = acc_ref[g]
        acc = acc + pltpu.roll(acc, HEAD_SIZE, 1)
        total = sum_ref[g]
        some = total > 0.0
        safe = jnp.where(some, total, 1.0)
        level = jnp.where(some, peak_ref[g] + jnp.log(safe), NEGATIVE)
        high = level.astype(jnp.bfloat16).astype(jnp.float32)
        middle = (level - high).astype(jnp.bfloat16).astype(jnp.float32)
        low = level - high - middle
        tail = jnp.where(out_lane == g, high, tail)
        tail = jnp.where(out_lane == heads + g, middle, tail)
        tail = jnp.where(out_lane == 2 * heads + g, low, tail)
        result = acc / safe
        if g % 2 == 0:
            left = result
        if g % 2 == 1 or g == heads - 1:
            block = jnp.where(out_lane < HEAD_SIZE, left, result)
            out_ref[0, :, g // 2 * 128 : g // 2 * 128 + 128] = block.astype(out_ref.dtype)
    out_ref[0, :, out_ref.shape[2] - 128 :] = tail.astype(out_ref.dtype)


def attend(info, query, keys, values, fresh_key, fresh_value, rows, local_q):
    local_kv, pairs = keys.shape[1], keys.shape[2]
    group = local_q // local_kv
    per = FRESH_TOKENS // rows
    dests = query.shape[0] // rows
    cache_spec = pl.BlockSpec((1, local_kv, pairs, 128), lambda d, info: (d // per, 0, 0, 0))
    fresh_spec = pl.BlockSpec((local_kv, rows, 128), lambda d, info: (0, 0, 0))
    columns = (local_q + 1) // 2 * 128 + 128
    return pl.pallas_call(
        functools.partial(attend_kernel, group),
        grid_spec=pltpu.PrefetchScalarGridSpec(
            num_scalar_prefetch=1,
            grid=(dests,),
            in_specs=[
                pl.BlockSpec((rows, local_q * HEAD_SIZE), lambda d, info: (d, 0)),
                cache_spec,
                cache_spec,
                fresh_spec,
                fresh_spec,
            ],
            out_specs=pl.BlockSpec((1, rows, columns), lambda d, info: (d, 0, 0)),
            scratch_shapes=[pltpu.VMEM((local_q, rows, 128), jnp.float32)] * 3,
        ),
        out_shape=jax.ShapeDtypeStruct((dests, rows, columns), jnp.bfloat16),
        compiler_params=pltpu.CompilerParams(vmem_limit_bytes=40 * 1024 * 1024),
        cost_estimate=pl.CostEstimate(
            flops=8 * query.size * pairs * 2, bytes_accessed=16 << 20, transcendentals=query.size * pairs // 32
        ),
    )(info, query, keys, values, fresh_key, fresh_value)


def swap_cores(values):
    count = lax.axis_size("tp")
    return lax.ppermute(values, "tp", [(i, i ^ 1) for i in range(count)])


def sum_halves(mine, others):
    received = swap_cores(others.astype(jnp.bfloat16)).astype(jnp.float32)
    return (mine + received).astype(jnp.bfloat16)


def sum_chips(values):
    count = lax.axis_size("tp")
    step = 2
    total = values.astype(jnp.float32)
    while step < count:
        sent = total.astype(jnp.bfloat16)
        received = lax.ppermute(sent, "tp", [(i, i ^ step) for i in range(count)])
        total = sent.astype(jnp.float32) + received.astype(jnp.float32)
        step = step * 2
    return total.astype(jnp.bfloat16)


def join_halves(values, core):
    other = swap_cores(values)
    first = jnp.where(core == 0, values, other)
    second = jnp.where(core == 0, other, values)
    return jnp.concatenate([first, second], axis=1)


def per_device(
    tokens,
    norm1_gain,
    w_query,
    key_weight,
    value_weight,
    rotated_key_cache,
    stored_value_cache,
    cache_len,
    w_out,
    norm2_gain,
    w_router,
    expert_ids,
    w_gate_up,
    w_down,
):
    tok_rows, width = tokens.shape
    seq_pos = lax.axis_index("seq")
    tp_pos = lax.axis_index("tp")
    local_q = w_query.shape[0] // HEAD_SIZE
    local_kv = key_weight.shape[0] // HEAD_SIZE
    requests = rotated_key_cache.shape[0]
    span = rotated_key_cache.shape[2] // HEAD_SIZE
    inputs = tokens.astype(jnp.float32)
    devices = lax.axis_size("seq")
    local_experts, _, own_width, hidden_size = w_gate_up.shape
    own_hidden = hidden_size // devices
    units = local_experts * own_hidden
    by_owner = jnp.transpose(
        w_gate_up.reshape(local_experts, 2, own_width, devices, own_hidden), (1, 3, 2, 0, 4)
    ).reshape(2, width, units)
    gate_rows = lax.all_to_all(by_owner[0], "seq", 0, 0, tiled=True)
    normalized_input = rms_norm(inputs, norm1_gain).astype(jnp.bfloat16)
    row_ids = seq_pos * tok_rows + jnp.arange(tok_rows, dtype=jnp.int32)
    owners = row_ids // FRESH_TOKENS
    positions = lookup(cache_len, owners) + row_ids % FRESH_TOKENS
    angle_position = positions.astype(jnp.float32)
    query_vector = apply_rotary(
        apply_projection(normalized_input, w_query).reshape(tok_rows, local_q, HEAD_SIZE),
        angle_position,
    ).astype(jnp.bfloat16)
    fresh_key = apply_rotary(
        apply_projection(normalized_input, key_weight).reshape(tok_rows, local_kv, HEAD_SIZE),
        angle_position,
    ).astype(jnp.bfloat16)
    fresh_value = (
        apply_projection(normalized_input, value_weight)
        .astype(jnp.bfloat16)
        .reshape(tok_rows, local_kv, HEAD_SIZE)
    )
    all_query = lax.all_gather(
        query_vector.reshape(tok_rows, local_q * HEAD_SIZE), "seq", axis=0, tiled=True
    )
    paired = (requests, local_kv, span // 2, 2 * HEAD_SIZE)
    pad = ((0, 0), (0, 0), (0, HEAD_SIZE))
    parts = attend(
        jnp.concatenate([seq_pos[None].astype(jnp.int32), cache_len]),
        all_query,
        rotated_key_cache.reshape(paired),
        stored_value_cache.reshape(paired),
        jnp.pad(jnp.transpose(fresh_key, (1, 0, 2)), pad),
        jnp.pad(jnp.transpose(fresh_value, (1, 0, 2)), pad),
        tok_rows,
        local_q,
    )
    parts, gate_rows = lax.optimization_barrier((parts, gate_rows))
    parts = lax.all_to_all(parts, "seq", 0, 0, tiled=True)
    parts, up_rows = lax.optimization_barrier((parts, by_owner[1]))
    up_rows = lax.all_to_all(up_rows, "seq", 0, 0, tiled=True)
    parts = parts.astype(jnp.float32)
    features = local_q * HEAD_SIZE
    tails = parts.shape[2] - 128
    pieces = parts[:, :, tails : tails + 3 * local_q]
    level = pieces[..., :local_q] + pieces[..., local_q : 2 * local_q] + pieces[..., 2 * local_q :]
    factor = jnp.exp(level - jnp.max(level, axis=0, keepdims=True))
    factor = factor / jnp.sum(factor, axis=0, keepdims=True)
    feature_head = jnp.arange(features, dtype=jnp.int32) // HEAD_SIZE
    widen = (jnp.arange(local_q, dtype=jnp.int32)[:, None] == feature_head[None, :]).astype(jnp.float32)
    factor = jnp.einsum("sth,hf->stf", factor, widen, precision=lax.Precision.HIGHEST)
    heads_out = jnp.sum(parts[:, :, :features] * factor, axis=0).astype(jnp.bfloat16)
    attn_part = jnp.dot(heads_out, w_out, preferred_element_type=jnp.float32)
    core = tp_pos % 2
    half = width // 2
    attn = sum_halves(
        lax.dynamic_slice_in_dim(attn_part, core * half, half, 1),
        lax.dynamic_slice_in_dim(attn_part, (1 - core) * half, half, 1),
    )
    attn = join_halves(sum_chips(attn), core).astype(jnp.float32)
    attn_out = attn.astype(jnp.bfloat16)
    normed2 = rms_norm(inputs + attn, norm2_gain).astype(jnp.bfloat16)
    logits = jnp.dot(normed2, w_router, preferred_element_type=jnp.float32)
    experts_all = w_router.shape[1]
    picked_all = expert_ids[:, :, None] == jnp.arange(experts_all, dtype=jnp.int32)[None, None, :]
    chosen = jnp.sum(jnp.where(picked_all, logits[:, None, :], 0.0), axis=-1)
    gates = jax.nn.softmax(chosen, axis=-1)
    local_ids = tp_pos * local_experts + jnp.arange(local_experts, dtype=jnp.int32)
    picked = expert_ids[:, :, None] == local_ids[None, None, :]
    share = jnp.sum(jnp.where(picked, gates[:, :, None], 0.0), axis=1)
    share_high = lax.reduce_precision(share, 8, 7)
    packed = jnp.concatenate(
        [
            lax.dynamic_slice_in_dim(normed2, core * half, half, 1),
            share_high.astype(jnp.bfloat16),
            (share - share_high).astype(jnp.bfloat16),
            jnp.zeros((tok_rows, 128 - 2 * local_experts), jnp.bfloat16),
        ],
        axis=1,
    )
    packed, up_rows = lax.optimization_barrier((packed, up_rows))
    packed = lax.all_gather(packed, "seq", axis=0, tiled=True)
    others = swap_cores(packed[:, :half])
    unit_expert = jnp.arange(units, dtype=jnp.int32) // own_hidden
    lanes = jnp.arange(128, dtype=jnp.int32)
    spread = (lanes[:, None] % local_experts == unit_expert[None, :]) & (lanes[:, None] < 2 * local_experts)
    share_all = jnp.dot(packed[:, half:], spread.astype(jnp.bfloat16), preferred_element_type=jnp.float32)

    def project(rows):
        mine = lax.dynamic_slice_in_dim(rows, core * half, half, 0)
        theirs = lax.dynamic_slice_in_dim(rows, (1 - core) * half, half, 0)
        return jnp.dot(packed[:, :half], mine, preferred_element_type=jnp.float32) + jnp.dot(
            others, theirs, preferred_element_type=jnp.float32
        )

    hidden = (jax.nn.silu(project(gate_rows)) * project(up_rows) * share_all).astype(jnp.bfloat16)
    down = w_down.reshape(units, width)
    down_mine = lax.dynamic_slice_in_dim(down, core * half, half, 1)
    down_others = lax.dynamic_slice_in_dim(down, (1 - core) * half, half, 1)
    moe_half = sum_halves(
        jnp.dot(hidden, down_mine, preferred_element_type=jnp.float32),
        jnp.dot(hidden, down_others, preferred_element_type=jnp.float32),
    )
    moe_half = lax.psum_scatter(moe_half, "seq", scatter_dimension=0, tiled=True)
    expert_out = join_halves(sum_chips(moe_half.astype(jnp.float32)), core)
    return (attn_out, expert_out)


def solution(mesh):
    return jax.shard_map(
        per_device,
        mesh=mesh,
        in_specs=(
            P("seq", None),
            P(),
            P("tp", None),
            P("tp", None),
            P("tp", None),
            P(None, "tp", "seq"),
            P(None, "tp", "seq"),
            P(),
            P("tp", None),
            P(),
            P(),
            P("seq", None),
            P("tp", None, "seq", None),
            P("tp", "seq", None),
        ),
        out_specs=(P("seq", None), P("seq", None)),
        check_vma=False,
    )
```

```python
import functools

import jax
import jax.numpy as jnp
from jax import lax
from jax.experimental import pallas as pl
from jax.experimental.pallas import tpu as pltpu
from jax.sharding import PartitionSpec as P

HEAD_SIZE = 64
FRESH_TOKENS = 512


EPS = 1e-05
THETA = 10000.0
NEGATIVE = -1e30


def rms_norm(values, gain):
    mean_square = jnp.mean(values * values, axis=-1, keepdims=True)
    return values * lax.rsqrt(mean_square + EPS) * gain.astype(values.dtype)


def apply_rotary(values, positions):
    half_dim = values.shape[-1] // 2
    exponent = jnp.arange(half_dim, dtype=jnp.float32) * (2.0 / values.shape[-1])
    freqs = THETA ** (-exponent)
    angles = positions[:, None] * freqs[None, :]
    cosine = jnp.cos(angles)[:, None, :]
    sine = jnp.sin(angles)[:, None, :]
    first = values[..., :half_dim]
    second = values[..., half_dim:]
    return jnp.concatenate(
        [first * cosine - second * sine, second * cosine + first * sine], axis=-1
    )


def apply_projection(normalized_input, weight):
    return jnp.einsum("td,fd->tf", normalized_input, weight, preferred_element_type=jnp.float32)


def lookup(table, index):
    hits = index[:, None] == jnp.arange(table.shape[0], dtype=jnp.int32)[None, :]
    return jnp.sum(jnp.where(hits, table[None, :], 0), axis=1)


def attend_kernel(group, info, q_ref, k_ref, v_ref, fk_ref, fv_ref, out_ref, peak_ref, sum_ref, acc_ref):
    heads, rows = acc_ref.shape[0], acc_ref.shape[1]
    pairs = k_ref.shape[2]
    columns = q_ref.shape[1]
    dest = pl.program_id(0)
    me = info[0]
    per = FRESH_TOKENS // rows
    length = info[1 + dest // per]
    base = me * (2 * pairs)
    col = lax.broadcasted_iota(jnp.int32, (columns, 128), 0)
    lane = lax.broadcasted_iota(jnp.int32, (columns, 128), 1)
    out_lane = lax.broadcasted_iota(jnp.int32, (rows, 128), 1)
    has_cache = base < length
    has_fresh = (dest // per == me // per) & (dest >= me)
    nt = (((1,), (1,)), ((), ()))

    def pick(g, odd):
        hit = (col == g * HEAD_SIZE + lane - odd * HEAD_SIZE) & (lane // HEAD_SIZE == odd)
        select = jnp.where(hit, HEAD_SIZE ** (-0.5), 0.0).astype(jnp.bfloat16)
        return jnp.dot(q_ref[...], select, preferred_element_type=jnp.float32).astype(jnp.bfloat16)

    @pl.when(jnp.logical_not(has_cache))
    def _():
        peak_ref[...] = jnp.full_like(peak_ref, NEGATIVE)
        sum_ref[...] = jnp.zeros_like(sum_ref)
        acc_ref[...] = jnp.zeros_like(acc_ref)

    @pl.when(has_cache)
    def _():
        even_pos = base + 2 * lax.broadcasted_iota(jnp.int32, (1, pairs), 1)
        even_bias = jnp.where(even_pos < length, 0.0, NEGATIVE)
        odd_bias = jnp.where(even_pos + 1 < length, 0.0, NEGATIVE)
        @pl.loop(0, heads // group)
        def _(j):
            for i in range(group):
                g = j * group + i
                keys = k_ref[0, j]
                values = v_ref[0, j]
                even = lax.dot_general(pick(g, 0), keys, nt, preferred_element_type=jnp.float32) + even_bias
                odd = lax.dot_general(pick(g, 1), keys, nt, preferred_element_type=jnp.float32) + odd_bias
                peak = jnp.max(jnp.maximum(even, odd), axis=1, keepdims=True)
                even = jnp.exp(even - peak)
                odd = jnp.exp(odd - peak)
                total = jnp.sum(even + odd, axis=1, keepdims=True)
                mix_even = jnp.dot(even.astype(jnp.bfloat16), values, preferred_element_type=jnp.float32)
                mix_odd = jnp.dot(odd.astype(jnp.bfloat16), values, preferred_element_type=jnp.float32)
                mixed = jnp.where(out_lane < HEAD_SIZE, mix_even, mix_odd)
                peak_ref[g] = jnp.broadcast_to(peak, (rows, 128))
                sum_ref[g] = jnp.broadcast_to(total, (rows, 128))
                acc_ref[g] = mixed

    @pl.when(has_fresh)
    def _():
        row_q = dest * rows + lax.broadcasted_iota(jnp.int32, (rows, rows), 0)
        row_k = me * rows + lax.broadcasted_iota(jnp.int32, (rows, rows), 1)
        bias = jnp.where(row_k <= row_q, 0.0, NEGATIVE)
        @pl.loop(0, heads // group)
        def _(j):
            for i in range(group):
                g = j * group + i
                score = lax.dot_general(pick(g, 0), fk_ref[j], nt, preferred_element_type=jnp.float32) + bias
                old = peak_ref[g][:, :1]
                peak = jnp.maximum(old, jnp.max(score, axis=1, keepdims=True))
                weight = jnp.exp(score - peak)
                factor = jnp.exp(old - peak)
                total = sum_ref[g][:, :1] * factor + jnp.sum(weight, axis=1, keepdims=True)
                mix = jnp.dot(weight.astype(jnp.bfloat16), fv_ref[j], preferred_element_type=jnp.float32)
                acc_ref[g] = acc_ref[g] * factor + mix
                peak_ref[g] = jnp.broadcast_to(peak, (rows, 128))
                sum_ref[g] = jnp.broadcast_to(total, (rows, 128))

    tail = jnp.zeros((rows, 128), jnp.float32)
    left = None
    for g in range(heads):
        acc = acc_ref[g]
        acc = acc + pltpu.roll(acc, HEAD_SIZE, 1)
        total = sum_ref[g]
        some = total > 0.0
        safe = jnp.where(some, total, 1.0)
        level = jnp.where(some, peak_ref[g] + jnp.log(safe), NEGATIVE)
        high = level.astype(jnp.bfloat16).astype(jnp.float32)
        middle = (level - high).astype(jnp.bfloat16).astype(jnp.float32)
        low = level - high - middle
        tail = jnp.where(out_lane == g, high, tail)
        tail = jnp.where(out_lane == heads + g, middle, tail)
        tail = jnp.where(out_lane == 2 * heads + g, low, tail)
        result = acc / safe
        if g % 2 == 0:
            left = result
        if g % 2 == 1 or g == heads - 1:
            block = jnp.where(out_lane < HEAD_SIZE, left, result)
            out_ref[0, :, g // 2 * 128 : g // 2 * 128 + 128] = block.astype(out_ref.dtype)
    out_ref[0, :, out_ref.shape[2] - 128 :] = tail.astype(out_ref.dtype)


def attend(info, query, keys, values, fresh_key, fresh_value, rows, local_q):
    local_kv, pairs = keys.shape[1], keys.shape[2]
    group = local_q // local_kv
    per = FRESH_TOKENS // rows
    dests = query.shape[0] // rows
    cache_spec = pl.BlockSpec((1, local_kv, pairs, 128), lambda d, info: (d // per, 0, 0, 0))
    fresh_spec = pl.BlockSpec((local_kv, rows, 128), lambda d, info: (0, 0, 0))
    columns = (local_q + 1) // 2 * 128 + 128
    return pl.pallas_call(
        functools.partial(attend_kernel, group),
        grid_spec=pltpu.PrefetchScalarGridSpec(
            num_scalar_prefetch=1,
            grid=(dests,),
            in_specs=[
                pl.BlockSpec((rows, local_q * HEAD_SIZE), lambda d, info: (d, 0)),
                cache_spec,
                cache_spec,
                fresh_spec,
                fresh_spec,
            ],
            out_specs=pl.BlockSpec((1, rows, columns), lambda d, info: (d, 0, 0)),
            scratch_shapes=[pltpu.VMEM((local_q, rows, 128), jnp.float32)] * 3,
        ),
        out_shape=jax.ShapeDtypeStruct((dests, rows, columns), jnp.bfloat16),
        compiler_params=pltpu.CompilerParams(vmem_limit_bytes=40 * 1024 * 1024),
        cost_estimate=pl.CostEstimate(
            flops=8 * query.size * pairs * 2, bytes_accessed=16 << 20, transcendentals=query.size * pairs // 32
        ),
    )(info, query, keys, values, fresh_key, fresh_value)


def swap_cores(values):
    count = lax.axis_size("tp")
    return lax.ppermute(values, "tp", [(i, i ^ 1) for i in range(count)])


def sum_halves(mine, others):
    received = swap_cores(others.astype(jnp.bfloat16)).astype(jnp.float32)
    return (mine + received).astype(jnp.bfloat16)


def sum_chips(values):
    count = lax.axis_size("tp")
    step = 2
    total = values.astype(jnp.float32)
    while step < count:
        sent = total.astype(jnp.bfloat16)
        received = lax.ppermute(sent, "tp", [(i, i ^ step) for i in range(count)])
        total = sent.astype(jnp.float32) + received.astype(jnp.float32)
        step = step * 2
    return total.astype(jnp.bfloat16)


def join_halves(values, core):
    other = swap_cores(values)
    first = jnp.where(core == 0, values, other)
    second = jnp.where(core == 0, other, values)
    return jnp.concatenate([first, second], axis=1)


def per_device(
    tokens,
    norm1_gain,
    w_query,
    key_weight,
    value_weight,
    rotated_key_cache,
    stored_value_cache,
    cache_len,
    w_out,
    norm2_gain,
    w_router,
    expert_ids,
    w_gate_up,
    w_down,
):
    tok_rows, width = tokens.shape
    seq_pos = lax.axis_index("seq")
    tp_pos = lax.axis_index("tp")
    local_q = w_query.shape[0] // HEAD_SIZE
    local_kv = key_weight.shape[0] // HEAD_SIZE
    requests = rotated_key_cache.shape[0]
    span = rotated_key_cache.shape[2] // HEAD_SIZE
    inputs = tokens.astype(jnp.float32)
    devices = lax.axis_size("seq")
    local_experts, _, own_width, hidden_size = w_gate_up.shape
    own_hidden = hidden_size // devices
    normalized_input = rms_norm(inputs, norm1_gain).astype(jnp.bfloat16)
    row_ids = seq_pos * tok_rows + jnp.arange(tok_rows, dtype=jnp.int32)
    owners = row_ids // FRESH_TOKENS
    positions = lookup(cache_len, owners) + row_ids % FRESH_TOKENS
    angle_position = positions.astype(jnp.float32)
    query_vector = apply_rotary(
        apply_projection(normalized_input, w_query).reshape(tok_rows, local_q, HEAD_SIZE),
        angle_position,
    ).astype(jnp.bfloat16)
    units = local_experts * own_hidden
    by_owner = jnp.transpose(
        w_gate_up.reshape(local_experts, 2, own_width, devices, own_hidden), (3, 2, 1, 0, 4)
    ).reshape(width, 2 * units)
    fresh_key = apply_rotary(
        apply_projection(normalized_input, key_weight).reshape(tok_rows, local_kv, HEAD_SIZE),
        angle_position,
    ).astype(jnp.bfloat16)
    fresh_value = (
        apply_projection(normalized_input, value_weight)
        .astype(jnp.bfloat16)
        .reshape(tok_rows, local_kv, HEAD_SIZE)
    )
    all_query = lax.all_gather(
        query_vector.reshape(tok_rows, local_q * HEAD_SIZE), "seq", axis=0, tiled=True
    )
    all_query, by_owner = lax.optimization_barrier((all_query, by_owner))
    own_gate_up = lax.all_to_all(by_owner, "seq", 0, 0, tiled=True)
    paired = (requests, local_kv, span // 2, 2 * HEAD_SIZE)
    pad = ((0, 0), (0, 0), (0, HEAD_SIZE))
    parts = attend(
        jnp.concatenate([seq_pos[None].astype(jnp.int32), cache_len]),
        all_query,
        rotated_key_cache.reshape(paired),
        stored_value_cache.reshape(paired),
        jnp.pad(jnp.transpose(fresh_key, (1, 0, 2)), pad),
        jnp.pad(jnp.transpose(fresh_value, (1, 0, 2)), pad),
        tok_rows,
        local_q,
    )
    parts, own_gate_up = lax.optimization_barrier((parts, own_gate_up))
    parts = lax.all_to_all(parts, "seq", 0, 0, tiled=True)
    parts = parts.astype(jnp.float32)
    features = local_q * HEAD_SIZE
    tails = parts.shape[2] - 128
    pieces = parts[:, :, tails : tails + 3 * local_q]
    level = pieces[..., :local_q] + pieces[..., local_q : 2 * local_q] + pieces[..., 2 * local_q :]
    factor = jnp.exp(level - jnp.max(level, axis=0, keepdims=True))
    factor = factor / jnp.sum(factor, axis=0, keepdims=True)
    feature_head = jnp.arange(features, dtype=jnp.int32) // HEAD_SIZE
    widen = (jnp.arange(local_q, dtype=jnp.int32)[:, None] == feature_head[None, :]).astype(jnp.float32)
    factor = jnp.einsum("sth,hf->stf", factor, widen, precision=lax.Precision.HIGHEST)
    heads_out = jnp.sum(parts[:, :, :features] * factor, axis=0).astype(jnp.bfloat16)
    attn_part = jnp.dot(heads_out, w_out, preferred_element_type=jnp.float32)
    core = tp_pos % 2
    half = width // 2
    attn = sum_halves(
        lax.dynamic_slice_in_dim(attn_part, core * half, half, 1),
        lax.dynamic_slice_in_dim(attn_part, (1 - core) * half, half, 1),
    )
    attn = join_halves(sum_chips(attn), core).astype(jnp.float32)
    attn_out = attn.astype(jnp.bfloat16)
    normed2 = rms_norm(inputs + attn, norm2_gain).astype(jnp.bfloat16)
    logits = jnp.dot(normed2, w_router, preferred_element_type=jnp.float32)
    experts_all = w_router.shape[1]
    picked_all = expert_ids[:, :, None] == jnp.arange(experts_all, dtype=jnp.int32)[None, None, :]
    chosen = jnp.sum(jnp.where(picked_all, logits[:, None, :], 0.0), axis=-1)
    gates = jax.nn.softmax(chosen, axis=-1)
    local_ids = tp_pos * local_experts + jnp.arange(local_experts, dtype=jnp.int32)
    picked = expert_ids[:, :, None] == local_ids[None, None, :]
    share = jnp.sum(jnp.where(picked, gates[:, :, None], 0.0), axis=1)
    share_high = lax.reduce_precision(share, 8, 7)
    packed = jnp.concatenate(
        [
            lax.dynamic_slice_in_dim(normed2, core * half, half, 1),
            share_high.astype(jnp.bfloat16),
            (share - share_high).astype(jnp.bfloat16),
            jnp.zeros((tok_rows, 128 - 2 * local_experts), jnp.bfloat16),
        ],
        axis=1,
    )
    packed = lax.all_gather(packed, "seq", axis=0, tiled=True)
    others = swap_cores(packed[:, :half])
    unit_expert = jnp.arange(units, dtype=jnp.int32) // own_hidden
    lanes = jnp.arange(128, dtype=jnp.int32)
    spread = (lanes[:, None] % local_experts == unit_expert[None, :]) & (lanes[:, None] < 2 * local_experts)
    share_all = jnp.dot(packed[:, half:], spread.astype(jnp.bfloat16), preferred_element_type=jnp.float32)
    gate_up_mine = lax.dynamic_slice_in_dim(own_gate_up, core * half, half, 0)
    gate_up_others = lax.dynamic_slice_in_dim(own_gate_up, (1 - core) * half, half, 0)
    both = jnp.dot(packed[:, :half], gate_up_mine, preferred_element_type=jnp.float32)
    both = both + jnp.dot(others, gate_up_others, preferred_element_type=jnp.float32)
    hidden = (jax.nn.silu(both[:, :units]) * both[:, units:] * share_all).astype(jnp.bfloat16)
    down = w_down.reshape(units, width)
    down_mine = lax.dynamic_slice_in_dim(down, core * half, half, 1)
    down_others = lax.dynamic_slice_in_dim(down, (1 - core) * half, half, 1)
    moe_half = sum_halves(
        jnp.dot(hidden, down_mine, preferred_element_type=jnp.float32),
        jnp.dot(hidden, down_others, preferred_element_type=jnp.float32),
    )
    moe_half = lax.psum_scatter(moe_half, "seq", scatter_dimension=0, tiled=True)
    expert_out = join_halves(sum_chips(moe_half.astype(jnp.float32)), core)
    return (attn_out, expert_out)


def solution(mesh):
    return jax.shard_map(
        per_device,
        mesh=mesh,
        in_specs=(
            P("seq", None),
            P(),
            P("tp", None),
            P("tp", None),
            P("tp", None),
            P(None, "tp", "seq"),
            P(None, "tp", "seq"),
            P(),
            P("tp", None),
            P(),
            P(),
            P("seq", None),
            P("tp", None, "seq", None),
            P("tp", "seq", None),
        ),
        out_specs=(P("seq", None), P("seq", None)),
        check_vma=False,
    )
```

```python
import functools

import jax
import jax.numpy as jnp
from jax import lax
from jax.experimental import pallas as pl
from jax.experimental.pallas import tpu as pltpu
from jax.sharding import PartitionSpec as P

HEAD_SIZE = 64
FRESH_TOKENS = 512


EPS = 1e-05
THETA = 10000.0
NEGATIVE = -1e30


def rms_norm(values, gain):
    mean_square = jnp.mean(values * values, axis=-1, keepdims=True)
    return values * lax.rsqrt(mean_square + EPS) * gain.astype(values.dtype)


def apply_rotary(values, positions):
    half_dim = values.shape[-1] // 2
    exponent = jnp.arange(half_dim, dtype=jnp.float32) * (2.0 / values.shape[-1])
    freqs = THETA ** (-exponent)
    angles = positions[:, None] * freqs[None, :]
    cosine = jnp.cos(angles)[:, None, :]
    sine = jnp.sin(angles)[:, None, :]
    first = values[..., :half_dim]
    second = values[..., half_dim:]
    return jnp.concatenate(
        [first * cosine - second * sine, second * cosine + first * sine], axis=-1
    )


def apply_projection(normalized_input, weight):
    return jnp.einsum("td,fd->tf", normalized_input, weight, preferred_element_type=jnp.float32)


def lookup(table, index):
    hits = index[:, None] == jnp.arange(table.shape[0], dtype=jnp.int32)[None, :]
    return jnp.sum(jnp.where(hits, table[None, :], 0), axis=1)


def attend_kernel(group, info, q_ref, k_ref, v_ref, fk_ref, fv_ref, out_ref, peak_ref, sum_ref, acc_ref):
    heads, rows = acc_ref.shape[0], acc_ref.shape[1]
    pairs = k_ref.shape[2]
    columns = q_ref.shape[1]
    dest = pl.program_id(0)
    me = info[0]
    per = FRESH_TOKENS // rows
    length = info[1 + dest // per]
    base = me * (2 * pairs)
    col = lax.broadcasted_iota(jnp.int32, (columns, 128), 0)
    lane = lax.broadcasted_iota(jnp.int32, (columns, 128), 1)
    out_lane = lax.broadcasted_iota(jnp.int32, (rows, 128), 1)
    has_cache = base < length
    has_fresh = (dest // per == me // per) & (dest >= me)
    nt = (((1,), (1,)), ((), ()))

    def pick(g, odd):
        hit = (col == g * HEAD_SIZE + lane - odd * HEAD_SIZE) & (lane // HEAD_SIZE == odd)
        select = jnp.where(hit, HEAD_SIZE ** (-0.5), 0.0).astype(jnp.bfloat16)
        return jnp.dot(q_ref[...], select, preferred_element_type=jnp.float32).astype(jnp.bfloat16)

    @pl.when(jnp.logical_not(has_cache))
    def _():
        peak_ref[...] = jnp.full_like(peak_ref, NEGATIVE)
        sum_ref[...] = jnp.zeros_like(sum_ref)
        acc_ref[...] = jnp.zeros_like(acc_ref)

    @pl.when(has_cache)
    def _():
        even_pos = base + 2 * lax.broadcasted_iota(jnp.int32, (1, pairs), 1)
        even_bias = jnp.where(even_pos < length, 0.0, NEGATIVE)
        odd_bias = jnp.where(even_pos + 1 < length, 0.0, NEGATIVE)
        @pl.loop(0, heads // group)
        def _(j):
            for i in range(group):
                g = j * group + i
                keys = k_ref[0, j]
                values = v_ref[0, j]
                even = lax.dot_general(pick(g, 0), keys, nt, preferred_element_type=jnp.float32) + even_bias
                odd = lax.dot_general(pick(g, 1), keys, nt, preferred_element_type=jnp.float32) + odd_bias
                peak = jnp.max(jnp.maximum(even, odd), axis=1, keepdims=True)
                even = jnp.exp(even - peak)
                odd = jnp.exp(odd - peak)
                total = jnp.sum(even + odd, axis=1, keepdims=True)
                mix_even = jnp.dot(even.astype(jnp.bfloat16), values, preferred_element_type=jnp.float32)
                mix_odd = jnp.dot(odd.astype(jnp.bfloat16), values, preferred_element_type=jnp.float32)
                mixed = jnp.where(out_lane < HEAD_SIZE, mix_even, mix_odd)
                peak_ref[g] = jnp.broadcast_to(peak, (rows, 128))
                sum_ref[g] = jnp.broadcast_to(total, (rows, 128))
                acc_ref[g] = mixed

    @pl.when(has_fresh)
    def _():
        row_q = dest * rows + lax.broadcasted_iota(jnp.int32, (rows, rows), 0)
        row_k = me * rows + lax.broadcasted_iota(jnp.int32, (rows, rows), 1)
        bias = jnp.where(row_k <= row_q, 0.0, NEGATIVE)
        @pl.loop(0, heads // group)
        def _(j):
            for i in range(group):
                g = j * group + i
                score = lax.dot_general(pick(g, 0), fk_ref[j], nt, preferred_element_type=jnp.float32) + bias
                old = peak_ref[g][:, :1]
                peak = jnp.maximum(old, jnp.max(score, axis=1, keepdims=True))
                weight = jnp.exp(score - peak)
                factor = jnp.exp(old - peak)
                total = sum_ref[g][:, :1] * factor + jnp.sum(weight, axis=1, keepdims=True)
                mix = jnp.dot(weight.astype(jnp.bfloat16), fv_ref[j], preferred_element_type=jnp.float32)
                acc_ref[g] = acc_ref[g] * factor + mix
                peak_ref[g] = jnp.broadcast_to(peak, (rows, 128))
                sum_ref[g] = jnp.broadcast_to(total, (rows, 128))

    tail = jnp.zeros((rows, 128), jnp.float32)
    left = None
    for g in range(heads):
        acc = acc_ref[g]
        acc = acc + pltpu.roll(acc, HEAD_SIZE, 1)
        total = sum_ref[g]
        some = total > 0.0
        safe = jnp.where(some, total, 1.0)
        level = jnp.where(some, peak_ref[g] + jnp.log(safe), NEGATIVE)
        high = level.astype(jnp.bfloat16).astype(jnp.float32)
        middle = (level - high).astype(jnp.bfloat16).astype(jnp.float32)
        low = level - high - middle
        tail = jnp.where(out_lane == g, high, tail)
        tail = jnp.where(out_lane == heads + g, middle, tail)
        tail = jnp.where(out_lane == 2 * heads + g, low, tail)
        result = acc / safe
        if g % 2 == 0:
            left = result
        if g % 2 == 1 or g == heads - 1:
            block = jnp.where(out_lane < HEAD_SIZE, left, result)
            out_ref[0, :, g // 2 * 128 : g // 2 * 128 + 128] = block.astype(out_ref.dtype)
    out_ref[0, :, out_ref.shape[2] - 128 :] = tail.astype(out_ref.dtype)


def attend(info, query, keys, values, fresh_key, fresh_value, rows, local_q):
    local_kv, pairs = keys.shape[1], keys.shape[2]
    group = local_q // local_kv
    per = FRESH_TOKENS // rows
    dests = query.shape[0] // rows
    cache_spec = pl.BlockSpec((1, local_kv, pairs, 128), lambda d, info: (d // per, 0, 0, 0))
    fresh_spec = pl.BlockSpec((local_kv, rows, 128), lambda d, info: (0, 0, 0))
    columns = (local_q + 1) // 2 * 128 + 128
    return pl.pallas_call(
        functools.partial(attend_kernel, group),
        grid_spec=pltpu.PrefetchScalarGridSpec(
            num_scalar_prefetch=1,
            grid=(dests,),
            in_specs=[
                pl.BlockSpec((rows, local_q * HEAD_SIZE), lambda d, info: (d, 0)),
                cache_spec,
                cache_spec,
                fresh_spec,
                fresh_spec,
            ],
            out_specs=pl.BlockSpec((1, rows, columns), lambda d, info: (d, 0, 0)),
            scratch_shapes=[pltpu.VMEM((local_q, rows, 128), jnp.float32)] * 3,
        ),
        out_shape=jax.ShapeDtypeStruct((dests, rows, columns), jnp.bfloat16),
        compiler_params=pltpu.CompilerParams(vmem_limit_bytes=40 * 1024 * 1024),
        cost_estimate=pl.CostEstimate(
            flops=8 * query.size * pairs * 2, bytes_accessed=16 << 20, transcendentals=query.size * pairs // 32
        ),
    )(info, query, keys, values, fresh_key, fresh_value)


def swap_cores(values):
    count = lax.axis_size("tp")
    return lax.ppermute(values, "tp", [(i, i ^ 1) for i in range(count)])


def sum_halves(mine, others):
    received = swap_cores(others.astype(jnp.bfloat16)).astype(jnp.float32)
    return (mine + received).astype(jnp.bfloat16)


def sum_chips(values):
    count = lax.axis_size("tp")
    step = 2
    total = values.astype(jnp.float32)
    while step < count:
        sent = total.astype(jnp.bfloat16)
        received = lax.ppermute(sent, "tp", [(i, i ^ step) for i in range(count)])
        total = sent.astype(jnp.float32) + received.astype(jnp.float32)
        step = step * 2
    return total.astype(jnp.bfloat16)


def join_halves(values, core):
    other = swap_cores(values)
    first = jnp.where(core == 0, values, other)
    second = jnp.where(core == 0, other, values)
    return jnp.concatenate([first, second], axis=1)


def per_device(
    tokens,
    norm1_gain,
    w_query,
    key_weight,
    value_weight,
    rotated_key_cache,
    stored_value_cache,
    cache_len,
    w_out,
    norm2_gain,
    w_router,
    expert_ids,
    w_gate_up,
    w_down,
):
    tok_rows, width = tokens.shape
    seq_pos = lax.axis_index("seq")
    tp_pos = lax.axis_index("tp")
    local_q = w_query.shape[0] // HEAD_SIZE
    local_kv = key_weight.shape[0] // HEAD_SIZE
    requests = rotated_key_cache.shape[0]
    span = rotated_key_cache.shape[2] // HEAD_SIZE
    inputs = tokens.astype(jnp.float32)
    devices = lax.axis_size("seq")
    local_experts, _, own_width, hidden_size = w_gate_up.shape
    own_hidden = hidden_size // devices
    normalized_input = rms_norm(inputs, norm1_gain).astype(jnp.bfloat16)
    row_ids = seq_pos * tok_rows + jnp.arange(tok_rows, dtype=jnp.int32)
    owners = row_ids // FRESH_TOKENS
    positions = lookup(cache_len, owners) + row_ids % FRESH_TOKENS
    angle_position = positions.astype(jnp.float32)
    query_vector = apply_rotary(
        apply_projection(normalized_input, w_query).reshape(tok_rows, local_q, HEAD_SIZE),
        angle_position,
    ).astype(jnp.bfloat16)
    units = local_experts * own_hidden
    by_owner = jnp.transpose(
        w_gate_up.reshape(local_experts, 2, own_width, devices, own_hidden), (3, 2, 1, 0, 4)
    ).reshape(devices, own_width, 2 * units)
    fresh_key = apply_rotary(
        apply_projection(normalized_input, key_weight).reshape(tok_rows, local_kv, HEAD_SIZE),
        angle_position,
    ).astype(jnp.bfloat16)
    fresh_value = (
        apply_projection(normalized_input, value_weight)
        .astype(jnp.bfloat16)
        .reshape(tok_rows, local_kv, HEAD_SIZE)
    )
    all_query = lax.all_gather(
        query_vector.reshape(tok_rows, local_q * HEAD_SIZE), "seq", axis=0, tiled=True
    )
    all_query, by_owner = lax.optimization_barrier((all_query, by_owner))
    own_gate_up = lax.all_to_all(by_owner, "seq", 0, 0, tiled=True).reshape(width, 2 * units)
    paired = (requests, local_kv, span // 2, 2 * HEAD_SIZE)
    pad = ((0, 0), (0, 0), (0, HEAD_SIZE))
    parts = attend(
        jnp.concatenate([seq_pos[None].astype(jnp.int32), cache_len]),
        all_query,
        rotated_key_cache.reshape(paired),
        stored_value_cache.reshape(paired),
        jnp.pad(jnp.transpose(fresh_key, (1, 0, 2)), pad),
        jnp.pad(jnp.transpose(fresh_value, (1, 0, 2)), pad),
        tok_rows,
        local_q,
    )
    parts, own_gate_up = lax.optimization_barrier((parts, own_gate_up))
    parts = lax.all_to_all(parts, "seq", 0, 0, tiled=True)
    parts = parts.astype(jnp.float32)
    features = local_q * HEAD_SIZE
    tails = parts.shape[2] - 128
    pieces = parts[:, :, tails : tails + 3 * local_q]
    level = pieces[..., :local_q] + pieces[..., local_q : 2 * local_q] + pieces[..., 2 * local_q :]
    factor = jnp.exp(level - jnp.max(level, axis=0, keepdims=True))
    factor = factor / jnp.sum(factor, axis=0, keepdims=True)
    feature_head = jnp.arange(features, dtype=jnp.int32) // HEAD_SIZE
    widen = (jnp.arange(local_q, dtype=jnp.int32)[:, None] == feature_head[None, :]).astype(jnp.float32)
    factor = jnp.einsum("sth,hf->stf", factor, widen, precision=lax.Precision.HIGHEST)
    heads_out = jnp.sum(parts[:, :, :features] * factor, axis=0).astype(jnp.bfloat16)
    attn_part = jnp.dot(heads_out, w_out, preferred_element_type=jnp.float32)
    core = tp_pos % 2
    half = width // 2
    attn = sum_halves(
        lax.dynamic_slice_in_dim(attn_part, core * half, half, 1),
        lax.dynamic_slice_in_dim(attn_part, (1 - core) * half, half, 1),
    )
    attn = join_halves(sum_chips(attn), core).astype(jnp.float32)
    attn_out = attn.astype(jnp.bfloat16)
    normed2 = rms_norm(inputs + attn, norm2_gain).astype(jnp.bfloat16)
    logits = jnp.dot(normed2, w_router, preferred_element_type=jnp.float32)
    experts_all = w_router.shape[1]
    picked_all = expert_ids[:, :, None] == jnp.arange(experts_all, dtype=jnp.int32)[None, None, :]
    chosen = jnp.sum(jnp.where(picked_all, logits[:, None, :], 0.0), axis=-1)
    gates = jax.nn.softmax(chosen, axis=-1)
    local_ids = tp_pos * local_experts + jnp.arange(local_experts, dtype=jnp.int32)
    picked = expert_ids[:, :, None] == local_ids[None, None, :]
    share = jnp.sum(jnp.where(picked, gates[:, :, None], 0.0), axis=1)
    share_high = lax.reduce_precision(share, 8, 7)
    packed = jnp.concatenate(
        [
            lax.dynamic_slice_in_dim(normed2, core * half, half, 1),
            share_high.astype(jnp.bfloat16),
            (share - share_high).astype(jnp.bfloat16),
            jnp.zeros((tok_rows, 128 - 2 * local_experts), jnp.bfloat16),
        ],
        axis=1,
    )
    packed = lax.all_gather(packed, "seq", axis=0, tiled=True)
    others = swap_cores(packed[:, :half])
    unit_expert = jnp.arange(units, dtype=jnp.int32) // own_hidden
    lanes = jnp.arange(128, dtype=jnp.int32)
    spread = (lanes[:, None] % local_experts == unit_expert[None, :]) & (lanes[:, None] < 2 * local_experts)
    share_all = jnp.dot(packed[:, half:], spread.astype(jnp.bfloat16), preferred_element_type=jnp.float32)
    gate_up_mine = lax.dynamic_slice_in_dim(own_gate_up, core * half, half, 0)
    gate_up_others = lax.dynamic_slice_in_dim(own_gate_up, (1 - core) * half, half, 0)
    both = jnp.dot(packed[:, :half], gate_up_mine, preferred_element_type=jnp.float32)
    both = both + jnp.dot(others, gate_up_others, preferred_element_type=jnp.float32)
    hidden = (jax.nn.silu(both[:, :units]) * both[:, units:] * share_all).astype(jnp.bfloat16)
    down = w_down.reshape(units, width)
    down_mine = lax.dynamic_slice_in_dim(down, core * half, half, 1)
    down_others = lax.dynamic_slice_in_dim(down, (1 - core) * half, half, 1)
    moe_half = sum_halves(
        jnp.dot(hidden, down_mine, preferred_element_type=jnp.float32),
        jnp.dot(hidden, down_others, preferred_element_type=jnp.float32),
    )
    moe_half = lax.psum_scatter(moe_half, "seq", scatter_dimension=0, tiled=True)
    expert_out = join_halves(sum_chips(moe_half.astype(jnp.float32)), core)
    return (attn_out, expert_out)


def solution(mesh):
    return jax.shard_map(
        per_device,
        mesh=mesh,
        in_specs=(
            P("seq", None),
            P(),
            P("tp", None),
            P("tp", None),
            P("tp", None),
            P(None, "tp", "seq"),
            P(None, "tp", "seq"),
            P(),
            P("tp", None),
            P(),
            P(),
            P("seq", None),
            P("tp", None, "seq", None),
            P("tp", "seq", None),
        ),
        out_specs=(P("seq", None), P("seq", None)),
        check_vma=False,
    )
```
